32 devices in a mesh: seq: 4 (over z), clip: 8 (over y, x, core).
Axes of the slice: x: 2, y: 2, z: 4, core: 2. Of those that a mesh axis runs over, the one named last changes fastest.
Arguments:
- clip_features: bfloat16 [8, 4, 8, 64, 384], P('clip', None, 'seq'), may hold values from -6 to 6
- enc_weight: bfloat16 [3, 3, 3, 384, 16], replicated, may hold values from -0.0625 to 0.0625
- noise_field: float32 [8, 4, 8, 64, 16], P('clip', None, 'seq'), may hold values from -6 to 6
- flow_times: int32 [8, 2], P('clip'), may hold values from 0 to 1000, as said below
- embed_weight: bfloat16 [64, 5120], replicated, may hold values from -0.75 to 0.75
- time_weight: bfloat16 [256, 5120], replicated, may hold values from -0.375 to 0.375
- norm_gain: float32 [5120], replicated, may hold values from 0.25 to 1.75
- qkv_weight: bfloat16 [5120, 3, 3072], P('clip', None, 'seq'), may hold values from -0.078125 to 0.078125
Outputs:
- attn_out: bfloat16 [8, 512, 3072], P('clip', 'seq')
- attn_tangent: bfloat16 [8, 512, 3072], P('clip', 'seq')
The draws below stay inside these ranges and needn't reach their ends.
Inputs may be any that keep to these rules, and one draw needn't show every extreme that they name: flow_times[c] = (index of r, index of t) with the index of r at most that of t; some clip has r index 0 and some t index 1000.
All inputs are finite; a program needn't handle non-finite values.
Results may differ from the reference program's by a relative error of at most 0.0044.
Values may be sent and summed in bfloat16 or wider, within the bound.
A program may use at most 128 MiB of HBM per device.

```python
import jax
import jax.numpy as jnp
from jax import lax

D = 5120
Z = 16
C = 384
HD = 128
HEADS = 24
TFEAT = 256
TGRID = 1000
FR = 4
WL = 64
INNER = 3072
PATCH = 64
HT = 8
CLIPS = 8


def draw_flow_times(key, part):
    key_one, key_two = jax.random.split(jax.random.fold_in(key, 17))
    draw_one = jax.random.randint(key_one, (CLIPS,), 0, TGRID + 1)
    draw_two = jax.random.randint(key_two, (CLIPS,), 0, TGRID + 1)
    start_idx = jnp.minimum(draw_one, draw_two).at[0].set(0)
    finish_idx = jnp.maximum(draw_one, draw_two).at[CLIPS - 1].set(TGRID)
    return jnp.stack([start_idx, finish_idx], axis=1).astype(jnp.int32)


def steps_of(key, shape, cuts, smallest, largest):
    def one(axis_at, blocks):
        steps = jax.random.uniform(jax.random.fold_in(jax.random.fold_in(key, 6), axis_at), (blocks,), jnp.float32, smallest / len(cuts), largest / len(cuts))
        return jnp.repeat(jnp.exp(steps), shape[axis_at] // blocks).reshape((-1,) + (1,) * (len(shape) - axis_at - 1))

    factor_of = one(*cuts[0])
    for cut in cuts[1:]:
        factor_of = factor_of * one(*cut)
    return factor_of


def scatter_about(own_key, shape, width, limit, pieces=(), kind=jnp.bfloat16):
    entries = jax.random.normal(own_key, shape, jnp.float32) * width
    if len(pieces) > 0:
        entries = steps_of(own_key, shape, pieces, -0.22, 0.18) * entries
    return jnp.clip(entries, min=-limit, max=limit).astype(kind)


def setup_inputs(seed: int = 0) -> dict:
    seeds = jax.random.split(jax.random.key(seed), 9)
    clip_features = scatter_about(seeds[0], (CLIPS, FR, HT, WL, C), 1.0, 6.0, ((0, 8), (2, 4)))
    enc_weight = scatter_about(seeds[1], (3, 3, 3, C, Z), (27 * C) ** -0.5, 0.0625)
    noise_field = scatter_about(seeds[2], (CLIPS, FR, HT, WL, Z), 1.0, 6.0, ((0, 8), (2, 4)), jnp.float32)
    flow_times = draw_flow_times(jax.random.fold_in(seeds[8], 71), 0)
    embed_weight = scatter_about(seeds[4], (PATCH, D), PATCH ** -0.5, 0.75)
    time_weight = scatter_about(seeds[5], (TFEAT, D), TFEAT ** -0.5, 0.375)
    norm_gain = jnp.clip(1.0 + 0.15 * jax.random.normal(seeds[6], (D,), jnp.float32), 0.25, 1.75)
    qkv_weight = scatter_about(seeds[7], (D, 3, INNER), D ** -0.5, 0.078125, ((0, 8), (2, 4)))
    return {"clip_features": clip_features, "enc_weight": enc_weight, "noise_field": noise_field, "flow_times": flow_times, "embed_weight": embed_weight, "time_weight": time_weight, "norm_gain": norm_gain, "qkv_weight": qkv_weight}


EPSILON = 1e-06

def time_features(flow_t, flow_h):
    quarter = TFEAT // 4
    freqs_omega = 8.0 * jnp.exp(-jnp.log(100.0) * jnp.arange(quarter, dtype=jnp.float32) / quarter)
    angle_t = freqs_omega * flow_t
    angle_h = freqs_omega * flow_h
    values = jnp.concatenate([jnp.sin(angle_t), jnp.cos(angle_t), jnp.sin(angle_h), jnp.cos(angle_h)])
    tangent = jnp.concatenate([freqs_omega * jnp.cos(angle_t), -freqs_omega * jnp.sin(angle_t), freqs_omega * jnp.cos(angle_h), -freqs_omega * jnp.sin(angle_h)])
    return (values[None, :], tangent[None, :])

def encode(padded, enc_weight):
    frames = padded.shape[0] - 2
    rows = padded.shape[1] - 2
    columns = padded.shape[2] - 2
    latent = jnp.zeros((frames, rows, columns, enc_weight.shape[4]), jnp.float32)
    for tap_time in range(3):
        for tap_row in range(3):
            for tap_col in range(3):
                window = padded[tap_time:tap_time + frames, tap_row:tap_row + rows, tap_col:tap_col + columns]
                latent = latent + jnp.einsum('fhwc,cz->fhwz', window.astype(jnp.float32), enc_weight[tap_time, tap_row, tap_col].astype(jnp.float32))
    return latent

def patchify(field):
    frames, rows, columns, chans = field.shape
    shaped = field.reshape(frames, rows // 2, 2, columns // 2, 2, chans)
    return shaped.transpose(1, 0, 3, 2, 4, 5).reshape(-1, 4 * chans)

def embed(patches, patch_tangent, values, tangent, embed_weight, time_weight, norm_gain):
    high = lax.Precision.HIGHEST
    embed_full = embed_weight.astype(jnp.float32)
    time_full = time_weight.astype(jnp.float32)
    hidden = jnp.dot(patches, embed_full, precision=high) + jnp.dot(values, time_full, precision=high)
    hidden_t = jnp.dot(patch_tangent, embed_full, precision=high) + jnp.dot(tangent, time_full, precision=high)
    inv_rms = lax.rsqrt(lax.optimization_barrier(jnp.mean(hidden * hidden, axis=-1, keepdims=True)) + EPSILON)
    cross = lax.optimization_barrier(jnp.mean(hidden * hidden_t, axis=-1, keepdims=True))
    normed = (hidden * inv_rms * norm_gain).astype(jnp.bfloat16)
    normed_t = (norm_gain * (hidden_t * inv_rms - hidden * inv_rms ** 3 * cross)).astype(jnp.bfloat16)
    return (normed, normed_t)

def attend(query, keys, vals, query_t, keys_t, vals_t):
    score_scale = query.shape[-1] ** (-0.5)
    qf, kf, vf = (query.astype(jnp.float32), keys.astype(jnp.float32), vals.astype(jnp.float32))
    qtf, ktf, vtf = (query_t.astype(jnp.float32), keys_t.astype(jnp.float32), vals_t.astype(jnp.float32))
    scores = jnp.einsum('hqd,hkd->hqk', qf, kf) * score_scale
    score_t = (jnp.einsum('hqd,hkd->hqk', qtf, kf) + jnp.einsum('hqd,hkd->hqk', qf, ktf)) * score_scale
    peak = lax.optimization_barrier(jnp.max(scores, axis=-1, keepdims=True))
    expo = jnp.exp(scores - peak)
    probs = expo / lax.optimization_barrier(jnp.sum(expo, axis=-1, keepdims=True))
    prob_t = probs * (score_t - lax.optimization_barrier(jnp.sum(probs * score_t, axis=-1, keepdims=True)))
    probs_b = probs.astype(jnp.bfloat16).astype(jnp.float32)
    prob_tb = prob_t.astype(jnp.bfloat16).astype(jnp.float32)
    output = jnp.einsum('hqk,hkd->hqd', probs_b, vf).astype(jnp.bfloat16)
    output_t = (jnp.einsum('hqk,hkd->hqd', prob_tb, vf) + jnp.einsum('hqk,hkd->hqd', probs_b, vtf)).astype(jnp.bfloat16)
    return (output, output_t)

def reference(clip_features, enc_weight, noise_field, flow_times, embed_weight, time_weight, norm_gain, qkv_weight):
    weight_flat = qkv_weight.reshape(D, 3 * HEADS * HD)

    def one_clip(inputs):
        feature_map, noise_one, pair = inputs
        padded = jnp.pad(feature_map, ((2, 0), (1, 1), (1, 1), (0, 0)))
        latent = encode(padded, enc_weight)
        start_t = pair[0].astype(jnp.float32) / TGRID
        flow_t = pair[1].astype(jnp.float32) / TGRID
        noisy = (1.0 - flow_t) * latent + flow_t * noise_one
        velocity = noise_one - latent
        values, tangent = time_features(flow_t, flow_t - start_t)
        normed, normed_t = embed(patchify(noisy), patchify(velocity), values, tangent, embed_weight, time_weight, norm_gain)
        projected = jnp.dot(normed, weight_flat, preferred_element_type=jnp.float32).astype(jnp.bfloat16)
        projected_t = jnp.dot(normed_t, weight_flat, preferred_element_type=jnp.float32).astype(jnp.bfloat16)
        tokens_all = normed.shape[0]
        heads_p = projected.reshape(tokens_all, 3, HEADS, HD).transpose(1, 2, 0, 3)
        heads_t = projected_t.reshape(tokens_all, 3, HEADS, HD).transpose(1, 2, 0, 3)
        output, output_t = attend(heads_p[0], heads_p[1], heads_p[2], heads_t[0], heads_t[1], heads_t[2])
        return (output.transpose(1, 0, 2).reshape(tokens_all, HEADS * HD), output_t.transpose(1, 0, 2).reshape(tokens_all, HEADS * HD))
    return lax.map(one_clip, (clip_features, noise_field, flow_times))
```

```python
import functools

import jax
import jax.numpy as jnp
import numpy as np
from jax import lax
from jax.experimental import pallas as pl
from jax.experimental.pallas import tpu as pltpu
from jax.sharding import PartitionSpec as P

HD = 128
TFEAT = 256
TGRID = 1000
EPSILON = 1e-06
LANES = 128
F32 = jnp.float32
BF16 = jnp.bfloat16


def time_features(flow_t, flow_h):
    quarter = TFEAT // 4
    omega = 8.0 * jnp.exp(-jnp.log(100.0) * jnp.arange(quarter, dtype=F32) / quarter)
    angle_t = omega * flow_t
    angle_h = omega * flow_h
    sin_t, cos_t, sin_h, cos_h = jnp.sin(angle_t), jnp.cos(angle_t), jnp.sin(angle_h), jnp.cos(angle_h)
    values = jnp.concatenate([sin_t, cos_t, sin_h, cos_h], axis=-1)
    tangent = jnp.concatenate([omega * cos_t, -omega * sin_t, omega * cos_h, -omega * sin_h], axis=-1)
    return values, tangent


def split(value, parts):
    terms = []
    for _ in range(parts):
        term = value.astype(BF16)
        terms.append(term)
        value = value - term.astype(F32)
    return terms


def dot(a, b):
    return jnp.dot(a, b, preferred_element_type=F32)


def dot_nt(a, b):
    return lax.dot_general(a, b, (((1,), (1,)), ((), ())), preferred_element_type=F32)


def conv_part(features, weight, frames, width, chans):
    pixels = features.shape[1]
    taps = [dot_nt(weight[...], features[f]) for f in range(frames)]
    lane = lax.broadcasted_iota(jnp.int32, (chans, pixels), 1)
    column = lax.rem(lane, width)
    block = 9 * chans
    own, edge = [], []
    for f in range(frames):
        acc = taps[f][2 * block : 3 * block]
        if f >= 1:
            acc = acc + taps[f - 1][block : 2 * block]
        if f >= 2:
            acc = acc + taps[f - 2][:block]
        rows = []
        for b in range(3):
            part = [acc[(b * 3 + e) * chans : (b * 3 + e + 1) * chans] for e in range(3)]
            total = part[1]
            total = total + jnp.where(column > 0, pltpu.roll(part[0], 1, 1), 0.0)
            total = total + jnp.where(column < width - 1, pltpu.roll(part[2], pixels - 1, 1), 0.0)
            rows.append(total)
        down = pltpu.roll(rows[0], width, 1)
        up = pltpu.roll(rows[2], pixels - width, 1)
        here = rows[1] + jnp.where(lane >= width, down, 0.0)
        own.append(here + jnp.where(lane < pixels - width, up, 0.0))
        edge.append(jnp.where(lane < width, down, up))
    return jnp.concatenate(own, axis=1), jnp.concatenate(edge, axis=1)


def tokens_part(latent, noise, pick, flow_t, chans):
    tokens = pick.shape[1] // 4
    terms = split(latent, 3) + split(noise, 3)
    moved = dot(jnp.concatenate(terms, axis=0), pick)
    lat = moved[:chans] + moved[chans : 2 * chans] + moved[2 * chans : 3 * chans]
    noi = moved[3 * chans : 4 * chans] + moved[4 * chans : 5 * chans] + moved[5 * chans :]
    noisy = (1.0 - flow_t) * lat + flow_t * noi
    velocity = noi - lat
    stacked = jnp.concatenate(
        [noisy[:, k * tokens : (k + 1) * tokens] for k in range(4)]
        + [velocity[:, k * tokens : (k + 1) * tokens] for k in range(4)],
        axis=0,
    )
    flipped = stacked.T
    return flipped[:, : 4 * chans], flipped[:, 4 * chans :]


def norm_part(noisy, velocity, embed_ref, time_rows, chunk):
    tokens, patch = noisy.shape
    depth = embed_ref.shape[1]
    lhs = jnp.concatenate(
        [jnp.concatenate(split(noisy, 3), axis=1), jnp.concatenate(split(velocity, 3), axis=1)], axis=0
    )
    square = jnp.zeros((tokens, chunk), F32)
    cross = jnp.zeros((tokens, chunk), F32)
    for k in range(depth // chunk):
        piece = embed_ref[:, k * chunk : (k + 1) * chunk]
        both = dot(lhs, jnp.concatenate([piece, piece, piece], axis=0))
        hidden = both[:tokens] + time_rows[0:1, k * chunk : (k + 1) * chunk]
        hidden_t = both[tokens:] + time_rows[1:2, k * chunk : (k + 1) * chunk]
        square = square + hidden * hidden
        cross = cross + hidden * hidden_t
    mean_sq = jnp.sum(square, axis=1, keepdims=True) / depth
    mean_cr = jnp.sum(cross, axis=1, keepdims=True) / depth
    inv = lax.rsqrt(mean_sq + EPSILON)
    shift = -(inv * inv * inv) * mean_cr
    inv_hi, inv_lo = [v.astype(F32) for v in split(inv, 2)]
    sh_hi, sh_lo = [v.astype(F32) for v in split(shift, 2)]
    lane = lax.broadcasted_iota(jnp.int32, (tokens, LANES - patch), 1)

    def tail(*columns):
        out = jnp.zeros((tokens, LANES - patch), F32)
        for index, column in enumerate(columns):
            out = jnp.where(lane == index, column, out)
        return out

    rows = jnp.concatenate([noisy * inv, tail(inv_hi, inv_lo, inv_hi)], axis=1)
    rows_t = jnp.concatenate(
        [velocity * inv + noisy * shift, tail(sh_hi, sh_lo, sh_hi, inv_hi, inv_lo, inv_hi)], axis=1
    )
    return rows.astype(BF16), rows_t.astype(BF16)


MESH = pl.DeviceIdType.MESH


def front_kernel(
    dims,
    f_ref, enc_ref, noise_ref, flow_ref, feats_ref, embed_ref, ecut_ref, gcut_ref, tcut_hbm, time_hbm, w_hbm, pick_ref,
    x_out, m_out,
    tcut_ref, time_ref, w_ref, load_sem,
    feats_buf, feats_send, feats_recv,
    edge_buf, before_buf, after_buf, edge_send, edge_recv,
    e_send, e_recv, tau_send, tau_recv, e_ss, e_rs, t_ss, t_rs,
    x_buf, x_ss, x_rs,
    g_buf, tau_buf, b_ss, b_rs, bt_ss, bt_rs, a_ss, a_rs, c_ss, c_rs,
):
    frames, width, chans, peers, clips = dims
    seq, clip = lax.axis_index("seq"), lax.axis_index("clip")
    patch, depth = embed_ref.shape
    share = ecut_ref.shape[1]
    part = w_ref.shape[2]
    chunk = patch // clips
    on_seq = [{"seq": lax.rem(seq + k, peers)} for k in range(1, peers)]
    on_clip = [{"clip": lax.rem(clip + k, clips)} for k in range(1, clips)]
    mate = {"clip": clip + 1 - 2 * lax.rem(clip, 2)}

    loads = [
        pltpu.make_async_copy(src, dst, load_sem.at[k])
        for k, (src, dst) in enumerate(((w_hbm, w_ref), (tcut_hbm, tcut_ref), (time_hbm, time_ref)))
    ]
    for load in loads:
        load.start()

    barrier = pltpu.get_barrier_semaphore()
    for who in on_seq + on_clip:
        pl.semaphore_signal(barrier, inc=1, device_id=who, device_id_type=MESH)
    pl.semaphore_wait(barrier, len(on_seq) + len(on_clip))
    sent = []

    def push(src, dst, ssem, rsem, who):
        copy = pltpu.make_async_remote_copy(
            src_ref=src, dst_ref=dst, send_sem=ssem, recv_sem=rsem, device_id=who, device_id_type=MESH
        )
        copy.start()
        sent.append(copy)
        return copy

    feats_in = [
        push(feats_ref, feats_buf.at[clip], feats_send.at[k], feats_recv.at[k], who) for k, who in enumerate(on_clip)
    ]
    feats_buf[clip] = feats_ref[...]

    own, edge = conv_part(f_ref, enc_ref, frames, width, chans)
    edge_buf[...] = edge

    def edge_copy(dst, k, step):
        return pltpu.make_async_remote_copy(
            src_ref=edge_buf, dst_ref=dst, send_sem=edge_send.at[k], recv_sem=edge_recv.at[k],
            device_id={"seq": lax.rem(seq + peers + step, peers)}, device_id_type=MESH,
        )

    to_next, to_last = edge_copy(before_buf, 0, 1), edge_copy(after_buf, 1, -1)

    @pl.when(seq < peers - 1)
    def _():
        to_next.start()

    @pl.when(seq > 0)
    def _():
        to_last.start()

    @pl.when(seq == 0)
    def _():
        before_buf[...] = jnp.zeros_like(before_buf)

    @pl.when(seq == peers - 1)
    def _():
        after_buf[...] = jnp.zeros_like(after_buf)

    gain = gcut_ref[...]
    left = jnp.concatenate(split(ecut_ref[...].astype(F32) * gain, 2), axis=0)
    loads[0].wait()
    for i in range(3):
        both = dot(left, w_ref[i])
        both = both[:patch] + both[patch:]
        for c in range(clips):
            e_send[c, :, i * part : (i + 1) * part] = both[c * chunk : (c + 1) * chunk]
    e_in = [
        push(e_send.at[lax.rem(clip + k + 1, clips)], e_recv.at[k], e_ss.at[k], e_rs.at[k], who)
        for k, who in enumerate(on_clip)
    ]
    for copy in feats_in:
        copy.wait_recv()
    loads[1].wait()
    feats = feats_buf[...].reshape(clips * 8, feats_buf.shape[2])
    both = dot(jnp.concatenate(split(feats, 2), axis=0), tcut_ref[...])
    left = jnp.concatenate(split((both[: clips * 8] + both[clips * 8 :]) * gain, 2), axis=0)
    for i in range(3):
        both = dot(left, w_ref[i])
        both = both[: clips * 8] + both[clips * 8 :]
        for c in range(clips):
            tau_send[c, :, i * part : (i + 1) * part] = both[c * 8 : c * 8 + 2]
    tau_in = [
        push(tau_send.at[lax.rem(clip + k + 1, clips)], tau_recv.at[k], t_ss.at[k], t_rs.at[k], who)
        for k, who in enumerate(on_clip)
    ]

    loads[2].wait()
    mine = jnp.concatenate(split(feats_ref[...], 2), axis=0)
    times = dot(mine, time_ref[...])
    times = times[:8] + times[8:]

    @pl.when(seq > 0)
    def _():
        to_next.wait_recv()

    @pl.when(seq < peers - 1)
    def _():
        to_last.wait_recv()

    pixels = f_ref.shape[1]
    lane = lax.rem(lax.broadcasted_iota(jnp.int32, own.shape, 1), pixels)
    latent = own + jnp.where(lane < width, before_buf[...], 0.0)
    latent = latent + jnp.where(lane >= pixels - width, after_buf[...], 0.0)
    noise = jnp.concatenate(
        [noise_ref[f, r] for f in range(frames) for r in range(noise_ref.shape[1])], axis=1
    )
    noisy, velocity = tokens_part(latent, noise, pick_ref[...], flow_ref[...], chans)
    rows, rows_t = norm_part(noisy, velocity, embed_ref, times, 512)
    x_buf[seq, 0] = rows
    x_buf[seq, 1] = rows_t
    x_in = [push(x_buf.at[seq], x_buf.at[seq], x_ss.at[k], x_rs.at[k], who) for k, who in enumerate(on_seq)]

    for copy in e_in:
        copy.wait_recv()
    total = e_send[clip]
    for k in range(clips - 1):
        total = total + e_recv[k]
    g_buf[clip, seq] = total.astype(BF16)
    b_in = [
        push(g_buf.at[clip, seq], g_buf.at[clip, seq], b_ss.at[k], b_rs.at[k], who) for k, who in enumerate(on_seq)
    ]
    for copy in tau_in:
        copy.wait_recv()
    total = tau_send[clip]
    for k in range(clips - 1):
        total = total + tau_recv[k]
    tau_buf[seq] = total
    bt_in = [
        push(tau_buf.at[seq], tau_buf.at[seq], bt_ss.at[k], bt_rs.at[k], who) for k, who in enumerate(on_seq)
    ]
    for copy in b_in:
        copy.wait_recv()
    c_in = [push(g_buf.at[clip], g_buf.at[clip], c_ss.at[0], c_rs.at[0], mate)]
    a_in = [
        push(g_buf.at[clip], g_buf.at[clip], a_ss.at[k], a_rs.at[k], on_clip[2 * k + 1])
        for k in range(clips // 2 - 1)
    ]
    for k, copy in enumerate(a_in):
        copy.wait_recv()
        src = lax.rem(clip + clips - 2 * (k + 1), clips)
        c_in.append(push(g_buf.at[src], g_buf.at[src], c_ss.at[k + 1], c_rs.at[k + 1], mate))
    for copy in bt_in + x_in + c_in:
        copy.wait_recv()
    for p in range(peers):
        x_out[0, p * x_buf.shape[2] : (p + 1) * x_buf.shape[2]] = x_buf[p, 0]
        x_out[1, p * x_buf.shape[2] : (p + 1) * x_buf.shape[2]] = x_buf[p, 1]
        for c in range(clips):
            m_out[p, c * chunk : (c + 1) * chunk] = g_buf[c, p]
        hi = tau_buf[p].astype(BF16).astype(F32)
        lo = tau_buf[p] - hi
        extra = [hi[0:1], hi[0:1], lo[0:1], hi[1:2], hi[1:2], lo[1:2]]
        row = lax.broadcasted_iota(jnp.int32, (LANES - patch, 3 * part), 0)
        tail = jnp.zeros((LANES - patch, 3 * part), F32)
        for index, value in enumerate(extra):
            tail = jnp.where(row == index, value, tail)
        m_out[p, patch:] = tail.astype(BF16)
    for copy in sent:
        copy.wait_send()

    @pl.when(seq < peers - 1)
    def _():
        to_next.wait_send()

    @pl.when(seq > 0)
    def _():
        to_last.wait_send()


def attend_kernel(per, x_ref, xt_ref, xo_ref, xto_ref, q_ref, k_ref, v_ref, out_ref, out_t_ref):
    scale = HD ** (-0.5)
    wq, wk, wv = q_ref[0], k_ref[0], v_ref[0]

    def project(rows_ref, weight):
        return dot(rows_ref[...], weight).astype(BF16)

    keys, keys_t = project(x_ref, wk), project(xt_ref, wk)
    vals, vals_t = project(x_ref, wv), project(xt_ref, wv)
    query, query_t = project(xo_ref, wq), project(xto_ref, wq)
    for h in range(per):
        at = slice(h * HD, (h + 1) * HD)
        q, qt, k, kt, v, vt = (m[:, at] for m in (query, query_t, keys, keys_t, vals, vals_t))
        scores = dot_nt(q, k) * scale
        score_t = dot_nt(jnp.concatenate([qt, q], axis=1), jnp.concatenate([k, kt], axis=1)) * scale
        expo = jnp.exp(scores - jnp.max(scores, axis=1, keepdims=True))
        probs = expo * (1.0 / jnp.sum(expo, axis=1, keepdims=True))
        prob_t = probs * (score_t - jnp.sum(probs * score_t, axis=1, keepdims=True))
        pb, ptb = probs.astype(BF16), prob_t.astype(BF16)
        out_ref[:, at] = dot(pb, v).astype(BF16)
        out_t_ref[:, at] = (dot(ptb, v) + dot(pb, vt)).astype(BF16)


VMEM = pl.BlockSpec(memory_space=pltpu.VMEM)


def attend(rows, rows_t, own, own_t, weights, inner):
    peers, depth, width = weights.shape
    part = width // 3
    per = 2 if (part // HD) % 2 == 0 else 1
    block = per * HD
    count = part // block
    tokens, total = own.shape[0], rows.shape[0]
    whole = lambda n: pl.BlockSpec((n, LANES), lambda i: (0, 0))
    spec = lambda g: pl.BlockSpec((1, depth, block), lambda i: (i // count, 0, g * count + i % count))
    out = pl.BlockSpec((tokens, block), lambda i: (0, i))
    shape = jax.ShapeDtypeStruct((tokens, inner), BF16)
    return pl.pallas_call(
        functools.partial(attend_kernel, per),
        grid=(peers * count,),
        out_shape=(shape, shape),
        in_specs=[whole(total), whole(total), whole(tokens), whole(tokens), spec(0), spec(1), spec(2)],
        out_specs=(out, out),
        name="attend",
    )(rows, rows_t, own, own_t, weights, weights, weights)


def local(clip_features, enc_weight, noise_field, flow_times, embed_weight, time_weight, norm_gain, qkv_weight):
    _, frames, rows, width, depth_c = clip_features.shape
    chans = enc_weight.shape[4]
    patch, depth = embed_weight.shape
    peers, clips = lax.axis_size("seq"), lax.axis_size("clip")
    share = qkv_weight.shape[0]
    part = qkv_weight.shape[2]
    pixels = rows * width
    tokens = frames * pixels // 4

    me = lax.axis_index("clip")
    gain = lax.dynamic_slice_in_dim(norm_gain, me * share, share, 0)[None, :]
    embed_cut = lax.dynamic_slice_in_dim(embed_weight, me * share, share, 1)
    time_cut = lax.dynamic_slice_in_dim(time_weight, me * share, share, 1)
    weight = qkv_weight.transpose(1, 0, 2)
    flow = flow_times.astype(F32) / TGRID
    values, tangent = time_features(flow[:, 1:2], flow[:, 1:2] - flow[:, 0:1])
    feats = jnp.concatenate([values, tangent, jnp.zeros((6, values.shape[1]), F32)], axis=0)
    features = clip_features.reshape(frames, pixels, depth_c)
    enc = enc_weight.transpose(0, 1, 2, 4, 3).reshape(27 * chans, depth_c)
    noise = noise_field[0].transpose(0, 1, 3, 2)
    i, f, j = np.meshgrid(np.arange(rows // 2), np.arange(frames), np.arange(width // 2), indexing="ij")
    source = np.stack(
        [((f * rows + 2 * i + p) * width + 2 * j + q).reshape(-1) for p in range(2) for q in range(2)]
    ).reshape(1, -1)
    pick = (jnp.arange(frames * pixels, dtype=jnp.int32)[:, None] == source.astype(np.int32)).astype(BF16)
    chunk = patch // clips
    dma = pltpu.SemaphoreType.DMA
    anywhere = pl.BlockSpec(memory_space=pl.ANY)
    edge = pltpu.VMEM((chans, frames * pixels), F32)
    gathered, weights = pl.pallas_call(
        functools.partial(front_kernel, (frames, width, chans, peers, clips)),
        out_shape=(
            jax.ShapeDtypeStruct((2, peers * tokens, LANES), BF16),
            jax.ShapeDtypeStruct((peers, LANES, 3 * part), BF16),
        ),
        in_specs=[VMEM] * 8 + [anywhere] * 3 + [VMEM],
        out_specs=(VMEM, VMEM),
        scratch_shapes=[
            pltpu.VMEM(time_cut.shape, BF16), pltpu.VMEM(time_weight.shape, BF16), pltpu.VMEM(weight.shape, BF16), dma((3,)),
            pltpu.VMEM((clips, 8, feats.shape[1]), F32), dma((clips - 1,)), dma((clips - 1,)),
            edge, edge, edge, dma((2,)), dma((2,)),
            pltpu.VMEM((clips, chunk, 3 * part), F32), pltpu.VMEM((clips - 1, chunk, 3 * part), F32),
            pltpu.VMEM((clips, 2, 3 * part), F32), pltpu.VMEM((clips - 1, 2, 3 * part), F32),
            dma((clips - 1,)), dma((clips - 1,)), dma((clips - 1,)), dma((clips - 1,)),
            pltpu.VMEM((peers, 2, tokens, LANES), BF16), dma((peers - 1,)), dma((peers - 1,)),
            pltpu.VMEM((clips, peers, chunk, 3 * part), BF16), pltpu.VMEM((peers, 2, 3 * part), F32),
            dma((peers - 1,)), dma((peers - 1,)), dma((peers - 1,)), dma((peers - 1,)),
            dma((clips // 2,)), dma((clips // 2,)), dma((clips // 2,)), dma((clips // 2,)),
        ],
        compiler_params=pltpu.CompilerParams(collective_id=0, has_side_effects=True),
        name="front",
    )(features, enc, noise, flow[:, 1:2], feats, embed_weight, embed_cut, gain, time_cut, time_weight, weight, pick)
    at = lax.axis_index("seq") * tokens
    x_own = lax.dynamic_slice_in_dim(gathered[0], at, tokens, 0)
    xt_own = lax.dynamic_slice_in_dim(gathered[1], at, tokens, 0)
    output, output_t = attend(gathered[0], gathered[1], x_own, xt_own, weights, peers * part)
    return output[None], output_t[None]


def solution(mesh):
    placed = (
        P("clip", None, "seq", None, None),
        P(),
        P("clip", None, "seq", None, None),
        P("clip", None),
        P(),
        P(),
        P(),
        P("clip", None, "seq"),
    )
    return jax.shard_map(
        local,
        mesh=mesh,
        in_specs=placed,
        out_specs=(P("clip", "seq", None), P("clip", "seq", None)),
        check_vma=False,
    )
```

```python
import functools

import jax
import jax.numpy as jnp
import numpy as np
from jax import lax
from jax.experimental import pallas as pl
from jax.experimental.pallas import tpu as pltpu
from jax.sharding import PartitionSpec as P

HD = 128
TFEAT = 256
TGRID = 1000
EPSILON = 1e-06
LANES = 128
F32 = jnp.float32
BF16 = jnp.bfloat16


def split(value, parts):
    terms = []
    for _ in range(parts):
        term = value.astype(BF16)
        terms.append(term)
        value = value - term.astype(F32)
    return terms


def dot(a, b):
    return jnp.dot(a, b, preferred_element_type=F32)


def dot_nt(a, b):
    return lax.dot_general(a, b, (((1,), (1,)), ((), ())), preferred_element_type=F32)


def conv_part(features, weight, frames, width, chans):
    pixels = features.shape[1]
    taps = [dot_nt(weight[...], features[f]) for f in range(frames)]
    lane = lax.broadcasted_iota(jnp.int32, (chans, pixels), 1)
    column = lax.rem(lane, width)
    block = 9 * chans
    own, edge = [], []
    for f in range(frames):
        acc = taps[f][2 * block : 3 * block]
        if f >= 1:
            acc = acc + taps[f - 1][block : 2 * block]
        if f >= 2:
            acc = acc + taps[f - 2][:block]
        rows = []
        for b in range(3):
            part = [acc[(b * 3 + e) * chans : (b * 3 + e + 1) * chans] for e in range(3)]
            total = part[1]
            total = total + jnp.where(column > 0, pltpu.roll(part[0], 1, 1), 0.0)
            total = total + jnp.where(column < width - 1, pltpu.roll(part[2], pixels - 1, 1), 0.0)
            rows.append(total)
        down = pltpu.roll(rows[0], width, 1)
        up = pltpu.roll(rows[2], pixels - width, 1)
        here = rows[1] + jnp.where(lane >= width, down, 0.0)
        own.append(here + jnp.where(lane < pixels - width, up, 0.0))
        edge.append(jnp.where(lane < width, down, up))
    return jnp.concatenate(own, axis=1), jnp.concatenate(edge, axis=1)


def tokens_part(latent, noise, pick, flow_t, chans):
    tokens = pick.shape[1] // 4
    terms = split(latent, 3) + split(noise, 3)
    moved = dot(jnp.concatenate(terms, axis=0), pick)
    lat = moved[:chans] + moved[chans : 2 * chans] + moved[2 * chans : 3 * chans]
    noi = moved[3 * chans : 4 * chans] + moved[4 * chans : 5 * chans] + moved[5 * chans :]
    noisy = (1.0 - flow_t) * lat + flow_t * noi
    velocity = noi - lat
    stacked = jnp.concatenate(
        [noisy[:, k * tokens : (k + 1) * tokens] for k in range(4)]
        + [velocity[:, k * tokens : (k + 1) * tokens] for k in range(4)],
        axis=0,
    )
    flipped = stacked.T
    return flipped[:, : 4 * chans], flipped[:, 4 * chans :]


def norm_part(noisy, velocity, embed_ref, time_rows, chunk):
    tokens, patch = noisy.shape
    depth = embed_ref.shape[1]
    lhs = jnp.concatenate(
        [jnp.concatenate(split(noisy, 3), axis=1), jnp.concatenate(split(velocity, 3), axis=1)], axis=0
    )
    square = jnp.zeros((tokens, chunk), F32)
    cross = jnp.zeros((tokens, chunk), F32)
    for k in range(depth // chunk):
        piece = embed_ref[:, k * chunk : (k + 1) * chunk]
        both = dot(lhs, jnp.concatenate([piece, piece, piece], axis=0))
        hidden = both[:tokens] + time_rows[0:1, k * chunk : (k + 1) * chunk]
        hidden_t = both[tokens:] + time_rows[1:2, k * chunk : (k + 1) * chunk]
        square = square + hidden * hidden
        cross = cross + hidden * hidden_t
    mean_sq = jnp.sum(square, axis=1, keepdims=True) / depth
    mean_cr = jnp.sum(cross, axis=1, keepdims=True) / depth
    inv = lax.rsqrt(mean_sq + EPSILON)
    shift = -(inv * inv * inv) * mean_cr
    inv_hi, inv_lo = [v.astype(F32) for v in split(inv, 2)]
    sh_hi, sh_lo = [v.astype(F32) for v in split(shift, 2)]
    lane = lax.broadcasted_iota(jnp.int32, (tokens, LANES - patch), 1)

    def tail(*columns):
        out = jnp.zeros((tokens, LANES - patch), F32)
        for index, column in enumerate(columns):
            out = jnp.where(lane == index, column, out)
        return out

    rows = jnp.concatenate([noisy * inv, tail(inv_hi, inv_lo, inv_hi)], axis=1)
    rows_t = jnp.concatenate(
        [velocity * inv + noisy * shift, tail(sh_hi, sh_lo, sh_hi, inv_hi, inv_lo, inv_hi)], axis=1
    )
    return rows.astype(BF16), rows_t.astype(BF16)


MESH = pl.DeviceIdType.MESH


def front_kernel(
    dims,
    flow_ref, source_ref, w_hbm, ecut_hbm, gcut_hbm, tcut_hbm, f_hbm, enc_hbm, time_hbm, noise_hbm, embed_hbm,
    x_out, xt_out, x_own, xt_own, m_out,
    w_ref, ecut_ref, gcut_ref, tcut_ref, f_ref, enc_ref, time_ref, noise_ref, embed_ref, load_sem, feats_ref,
    feats_buf, feats_send, feats_recv,
    edge_buf, before_buf, after_buf, edge_send, edge_recv,
    e_send, e_recv, tau_send, tau_recv, e_ss, e_rs, t_ss, t_rs,
    x_buf, x_ss, x_rs,
    g_buf, tau_buf, b_ss, b_rs, bt_ss, bt_rs, a_ss, a_rs, c_ss, c_rs,
):
    frames, width, chans, peers, clips = dims
    seq, clip = lax.axis_index("seq"), lax.axis_index("clip")
    patch, depth = embed_ref.shape
    share = ecut_ref.shape[1]
    part = w_ref.shape[2]
    chunk = patch // clips
    on_seq = [{"seq": lax.rem(seq + k, peers)} for k in range(1, peers)]
    on_clip = [{"clip": lax.rem(clip + k, clips)} for k in range(1, clips)]
    mate = {"clip": clip + 1 - 2 * lax.rem(clip, 2)}

    def cut(ref):
        if ref.shape[-1] == share:
            return ref
        return ref.at[:, pl.ds(pl.multiple_of(clip * share, share), share)]

    pairs = (
        (w_hbm, w_ref), (cut(ecut_hbm), ecut_ref), (cut(gcut_hbm), gcut_ref), (cut(tcut_hbm), tcut_ref),
        (f_hbm, f_ref), (enc_hbm, enc_ref), (time_hbm, time_ref), (noise_hbm, noise_ref), (embed_hbm, embed_ref),
    )
    loads = [pltpu.make_async_copy(src, dst, load_sem.at[k]) for k, (src, dst) in enumerate(pairs)]
    for load in loads:
        load.start()
    flow_r = flow_ref[0, 0].astype(F32) / TGRID
    flow_t = flow_ref[0, 1].astype(F32) / TGRID
    quarter = TFEAT // 4
    order = lax.broadcasted_iota(jnp.int32, (8, TFEAT), 1)
    line = lax.broadcasted_iota(jnp.int32, (8, TFEAT), 0)
    omega = 8.0 * jnp.exp(-np.float32(np.log(100.0)) * lax.rem(order, quarter).astype(F32) / quarter)
    angle = omega * jnp.where(order < 2 * quarter, flow_t, flow_t - flow_r)
    sine, cosine = jnp.sin(angle), jnp.cos(angle)
    first = lax.rem(order // quarter, 2) == 0
    feats_ref[...] = jnp.where(
        line == 0,
        jnp.where(first, sine, cosine),
        jnp.where(line == 1, jnp.where(first, omega * cosine, -omega * sine), 0.0),
    )

    barrier = pltpu.get_barrier_semaphore()
    for who in on_seq + on_clip:
        pl.semaphore_signal(barrier, inc=1, device_id=who, device_id_type=MESH)
    pl.semaphore_wait(barrier, len(on_seq) + len(on_clip))
    sent = []

    def push(src, dst, ssem, rsem, who):
        copy = pltpu.make_async_remote_copy(
            src_ref=src, dst_ref=dst, send_sem=ssem, recv_sem=rsem, device_id=who, device_id_type=MESH
        )
        copy.start()
        sent.append(copy)
        return copy

    feats_in = [
        push(feats_ref, feats_buf.at[clip], feats_send.at[k], feats_recv.at[k], who) for k, who in enumerate(on_clip)
    ]
    feats_buf[clip] = feats_ref[...]

    loads[1].wait()
    loads[2].wait()
    gain = gcut_ref[...]
    left = jnp.concatenate(split(ecut_ref[...].astype(F32) * gain, 2), axis=0)
    loads[0].wait()
    for i in range(3):
        both = dot(left, w_ref[i])
        both = both[:patch] + both[patch:]
        for c in range(clips):
            e_send[c, :, i * part : (i + 1) * part] = both[c * chunk : (c + 1) * chunk]
    e_in = [
        push(e_send.at[lax.rem(clip + k + 1, clips)], e_recv.at[k], e_ss.at[k], e_rs.at[k], who)
        for k, who in enumerate(on_clip)
    ]
    for copy in feats_in:
        copy.wait_recv()
    loads[3].wait()
    feats = feats_buf[...].reshape(clips * 8, feats_buf.shape[2])
    both = dot(jnp.concatenate(split(feats, 2), axis=0), tcut_ref[...])
    left = jnp.concatenate(split((both[: clips * 8] + both[clips * 8 :]) * gain, 2), axis=0)
    for i in range(3):
        both = dot(left, w_ref[i])
        both = both[: clips * 8] + both[clips * 8 :]
        for c in range(clips):
            tau_send[c, :, i * part : (i + 1) * part] = both[c * 8 : c * 8 + 2]
    tau_in = [
        push(tau_send.at[lax.rem(clip + k + 1, clips)], tau_recv.at[k], t_ss.at[k], t_rs.at[k], who)
        for k, who in enumerate(on_clip)
    ]

    loads[4].wait()
    loads[5].wait()
    own, edge = conv_part(f_ref, enc_ref, frames, width, chans)
    edge_buf[...] = edge

    def edge_copy(dst, k, step):
        return pltpu.make_async_remote_copy(
            src_ref=edge_buf, dst_ref=dst, send_sem=edge_send.at[k], recv_sem=edge_recv.at[k],
            device_id={"seq": lax.rem(seq + peers + step, peers)}, device_id_type=MESH,
        )

    to_next, to_last = edge_copy(before_buf, 0, 1), edge_copy(after_buf, 1, -1)

    @pl.when(seq < peers - 1)
    def _():
        to_next.start()

    @pl.when(seq > 0)
    def _():
        to_last.start()

    @pl.when(seq == 0)
    def _():
        before_buf[...] = jnp.zeros_like(before_buf)

    @pl.when(seq == peers - 1)
    def _():
        after_buf[...] = jnp.zeros_like(after_buf)

    loads[6].wait()
    mine = jnp.concatenate(split(feats_ref[...], 2), axis=0)
    times = dot(mine, time_ref[...])
    times = times[:8] + times[8:]

    for copy in e_in:
        copy.wait_recv()
    total = e_send[clip]
    for k in range(clips - 1):
        total = total + e_recv[k]
    g_buf[clip, seq] = total.astype(BF16)
    b_in = [
        push(g_buf.at[clip, seq], g_buf.at[clip, seq], b_ss.at[k], b_rs.at[k], who) for k, who in enumerate(on_seq)
    ]
    for copy in tau_in:
        copy.wait_recv()
    total = tau_send[clip]
    for k in range(clips - 1):
        total = total + tau_recv[k]
    tau_buf[seq] = total
    bt_in = [
        push(tau_buf.at[seq], tau_buf.at[seq], bt_ss.at[k], bt_rs.at[k], who) for k, who in enumerate(on_seq)
    ]
    @pl.when(seq > 0)
    def _():
        to_next.wait_recv()

    @pl.when(seq < peers - 1)
    def _():
        to_last.wait_recv()

    pixels = f_ref.shape[1]
    lane = lax.rem(lax.broadcasted_iota(jnp.int32, own.shape, 1), pixels)
    latent = own + jnp.where(lane < width, before_buf[...], 0.0)
    latent = latent + jnp.where(lane >= pixels - width, after_buf[...], 0.0)
    loads[7].wait()
    loads[8].wait()
    noise = jnp.concatenate(
        [noise_ref[f, r] for f in range(frames) for r in range(noise_ref.shape[1])], axis=1
    )
    places = lax.broadcasted_iota(jnp.int32, (own.shape[1], source_ref.shape[1]), 0)
    pick = (places == source_ref[...]).astype(F32).astype(BF16)
    noisy, velocity = tokens_part(latent, noise, pick, flow_t, chans)
    rows, rows_t = norm_part(noisy, velocity, embed_ref, times, 512)
    x_buf[seq, 0] = rows
    x_buf[seq, 1] = rows_t
    x_in = [push(x_buf.at[seq], x_buf.at[seq], x_ss.at[k], x_rs.at[k], who) for k, who in enumerate(on_seq)]

    for copy in b_in:
        copy.wait_recv()
    c_in = [push(g_buf.at[clip], g_buf.at[clip], c_ss.at[0], c_rs.at[0], mate)]
    a_in = [
        push(g_buf.at[clip], g_buf.at[clip], a_ss.at[k], a_rs.at[k], on_clip[2 * k + 1])
        for k in range(clips // 2 - 1)
    ]
    for k, copy in enumerate(a_in):
        copy.wait_recv()
        src = lax.rem(clip + clips - 2 * (k + 1), clips)
        c_in.append(push(g_buf.at[src], g_buf.at[src], c_ss.at[k + 1], c_rs.at[k + 1], mate))
    for copy in bt_in + x_in + c_in:
        copy.wait_recv()
    x_own[...] = x_buf[seq, 0]
    xt_own[...] = x_buf[seq, 1]
    tokens = x_buf.shape[2]
    for p in range(peers):
        x_out[p * tokens : (p + 1) * tokens] = x_buf[p, 0]
        xt_out[p * tokens : (p + 1) * tokens] = x_buf[p, 1]
        for c in range(clips):
            m_out[p, c * chunk : (c + 1) * chunk] = g_buf[c, p]
        hi = tau_buf[p].astype(BF16).astype(F32)
        lo = tau_buf[p] - hi
        extra = [hi[0:1], hi[0:1], lo[0:1], hi[1:2], hi[1:2], lo[1:2]]
        row = lax.broadcasted_iota(jnp.int32, (LANES - patch, 3 * part), 0)
        tail = jnp.zeros((LANES - patch, 3 * part), F32)
        for index, value in enumerate(extra):
            tail = jnp.where(row == index, value, tail)
        m_out[p, patch:] = tail.astype(BF16)
    for copy in sent:
        copy.wait_send()

    @pl.when(seq < peers - 1)
    def _():
        to_next.wait_send()

    @pl.when(seq > 0)
    def _():
        to_last.wait_send()


def attend_kernel(per, x_ref, xt_ref, xo_ref, xto_ref, q_ref, k_ref, v_ref, out_ref, out_t_ref):
    scale = HD ** (-0.5)
    wq, wk, wv = q_ref[0], k_ref[0], v_ref[0]

    def project(rows_ref, weight):
        return dot(rows_ref[...], weight).astype(BF16)

    keys, keys_t = project(x_ref, wk), project(xt_ref, wk)
    vals, vals_t = project(x_ref, wv), project(xt_ref, wv)
    query, query_t = project(xo_ref, wq), project(xto_ref, wq)
    for h in range(per):
        at = slice(h * HD, (h + 1) * HD)
        q, qt, k, kt, v, vt = (m[:, at] for m in (query, query_t, keys, keys_t, vals, vals_t))
        scores = dot_nt(q, k)
        score_t = dot_nt(jnp.concatenate([qt, q], axis=1), jnp.concatenate([k, kt], axis=1))
        expo = jnp.exp((scores - jnp.max(scores, axis=1, keepdims=True)) * scale)
        inv = 1.0 / jnp.sum(expo, axis=1, keepdims=True)
        mean = jnp.sum(expo * score_t, axis=1, keepdims=True) * inv
        eb, etb = expo.astype(BF16), (expo * (score_t - mean)).astype(BF16)
        out_ref[:, at] = (dot(eb, v) * inv).astype(BF16)
        out_t_ref[:, at] = (dot(etb, v) * (inv * scale) + dot(eb, vt) * inv).astype(BF16)


VMEM = pl.BlockSpec(memory_space=pltpu.VMEM)


def attend(rows, rows_t, own, own_t, weights, inner):
    peers, depth, width = weights.shape
    part = width // 3
    per = 2 if (part // HD) % 2 == 0 else 1
    block = per * HD
    count = part // block
    tokens, total = own.shape[0], rows.shape[0]
    whole = lambda n: pl.BlockSpec((n, LANES), lambda i: (0, 0))
    spec = lambda g: pl.BlockSpec((1, depth, block), lambda i: (i // count, 0, g * count + i % count))
    out = pl.BlockSpec((tokens, block), lambda i: (0, i))
    shape = jax.ShapeDtypeStruct((tokens, inner), BF16)
    return pl.pallas_call(
        functools.partial(attend_kernel, per),
        grid=(peers * count,),
        out_shape=(shape, shape),
        in_specs=[whole(total), whole(total), whole(tokens), whole(tokens), spec(0), spec(1), spec(2)],
        out_specs=(out, out),
        name="attend",
    )(rows, rows_t, own, own_t, weights, weights, weights)


def local(clip_features, enc_weight, noise_field, flow_times, embed_weight, time_weight, norm_gain, qkv_weight):
    _, frames, rows, width, depth_c = clip_features.shape
    chans = enc_weight.shape[4]
    patch, depth = embed_weight.shape
    peers, clips = lax.axis_size("seq"), lax.axis_size("clip")
    share = qkv_weight.shape[0]
    part = qkv_weight.shape[2]
    pixels = rows * width
    tokens = frames * pixels // 4

    gain, embed_cut, time_cut = norm_gain[None, :], embed_weight, time_weight
    if share % LANES:
        me = lax.axis_index("clip")
        gain, embed_cut, time_cut = (
            lax.dynamic_slice_in_dim(m, me * share, share, 1) for m in (gain, embed_weight, time_weight)
        )
    weight = qkv_weight.transpose(1, 0, 2)
    features = clip_features.reshape(frames, pixels, depth_c)
    enc = enc_weight.transpose(0, 1, 2, 4, 3).reshape(27 * chans, depth_c)
    noise = noise_field[0].transpose(0, 1, 3, 2)
    i, f, j = np.meshgrid(np.arange(rows // 2), np.arange(frames), np.arange(width // 2), indexing="ij")
    source = np.stack(
        [((f * rows + 2 * i + p) * width + 2 * j + q).reshape(-1) for p in range(2) for q in range(2)]
    ).reshape(1, -1)
    source = jnp.asarray(source.astype(np.int32))
    chunk = patch // clips
    dma = pltpu.SemaphoreType.DMA
    anywhere = pl.BlockSpec(memory_space=pl.ANY)
    edge = pltpu.VMEM((chans, frames * pixels), F32)
    x, xt, x_own, xt_own, weights = pl.pallas_call(
        functools.partial(front_kernel, (frames, width, chans, peers, clips)),
        out_shape=(
            jax.ShapeDtypeStruct((peers * tokens, LANES), BF16),
            jax.ShapeDtypeStruct((peers * tokens, LANES), BF16),
            jax.ShapeDtypeStruct((tokens, LANES), BF16),
            jax.ShapeDtypeStruct((tokens, LANES), BF16),
            jax.ShapeDtypeStruct((peers, LANES, 3 * part), BF16),
        ),
        in_specs=[pl.BlockSpec(memory_space=pltpu.SMEM), VMEM] + [anywhere] * 9,
        out_specs=(VMEM,) * 5,
        scratch_shapes=[
            pltpu.VMEM(weight.shape, BF16), pltpu.VMEM((patch, share), BF16), pltpu.VMEM((1, share), F32),
            pltpu.VMEM((TFEAT, share), BF16), pltpu.VMEM(features.shape, BF16), pltpu.VMEM(enc.shape, BF16),
            pltpu.VMEM(time_weight.shape, BF16), pltpu.VMEM(noise.shape, F32), pltpu.VMEM(embed_weight.shape, BF16),
            dma((9,)), pltpu.VMEM((8, TFEAT), F32),
            pltpu.VMEM((clips, 8, TFEAT), F32), dma((clips - 1,)), dma((clips - 1,)),
            edge, edge, edge, dma((2,)), dma((2,)),
            pltpu.VMEM((clips, chunk, 3 * part), F32), pltpu.VMEM((clips - 1, chunk, 3 * part), F32),
            pltpu.VMEM((clips, 2, 3 * part), F32), pltpu.VMEM((clips - 1, 2, 3 * part), F32),
            dma((clips - 1,)), dma((clips - 1,)), dma((clips - 1,)), dma((clips - 1,)),
            pltpu.VMEM((peers, 2, tokens, LANES), BF16), dma((peers - 1,)), dma((peers - 1,)),
            pltpu.VMEM((clips, peers, chunk, 3 * part), BF16), pltpu.VMEM((peers, 2, 3 * part), F32),
            dma((peers - 1,)), dma((peers - 1,)), dma((peers - 1,)), dma((peers - 1,)),
            dma((clips // 2,)), dma((clips // 2,)), dma((clips // 2,)), dma((clips // 2,)),
        ],
        compiler_params=pltpu.CompilerParams(collective_id=0, has_side_effects=True),
        name="front",
    )(flow_times, source, weight, embed_cut, gain, time_cut, features, enc, time_weight, noise, embed_weight)
    output, output_t = attend(x, xt, x_own, xt_own, weights, peers * part)
    return output[None], output_t[None]


def solution(mesh):
    placed = (
        P("clip", None, "seq", None, None),
        P(),
        P("clip", None, "seq", None, None),
        P("clip", None),
        P(),
        P(),
        P(),
        P("clip", None, "seq"),
    )
    return jax.shard_map(
        local,
        mesh=mesh,
        in_specs=placed,
        out_specs=(P("clip", "seq", None), P("clip", "seq", None)),
        check_vma=False,
    )
```

```python
import functools

import jax
import jax.numpy as jnp
import numpy as np
from jax import lax
from jax.experimental import pallas as pl
from jax.experimental.pallas import tpu as pltpu
from jax.sharding import PartitionSpec as P

HD = 128
TFEAT = 256
TGRID = 1000
EPSILON = 1e-06
LANES = 128
F32 = jnp.float32
BF16 = jnp.bfloat16


def split(value, parts):
    terms = []
    for _ in range(parts):
        term = value.astype(BF16)
        terms.append(term)
        value = value - term.astype(F32)
    return terms


def dot(a, b):
    return jnp.dot(a, b, preferred_element_type=F32)


def dot_nt(a, b):
    return lax.dot_general(a, b, (((1,), (1,)), ((), ())), preferred_element_type=F32)


def conv_part(features, weight, frames, width, chans):
    pixels = features.shape[1]
    taps = [dot_nt(weight[...], features[f]) for f in range(frames)]
    lane = lax.broadcasted_iota(jnp.int32, (chans, pixels), 1)
    column = lax.rem(lane, width)
    block = 9 * chans
    own, edge = [], []
    for f in range(frames):
        acc = taps[f][2 * block : 3 * block]
        if f >= 1:
            acc = acc + taps[f - 1][block : 2 * block]
        if f >= 2:
            acc = acc + taps[f - 2][:block]
        rows = []
        for b in range(3):
            part = [acc[(b * 3 + e) * chans : (b * 3 + e + 1) * chans] for e in range(3)]
            total = part[1]
            total = total + jnp.where(column > 0, pltpu.roll(part[0], 1, 1), 0.0)
            total = total + jnp.where(column < width - 1, pltpu.roll(part[2], pixels - 1, 1), 0.0)
            rows.append(total)
        down = pltpu.roll(rows[0], width, 1)
        up = pltpu.roll(rows[2], pixels - width, 1)
        here = rows[1] + jnp.where(lane >= width, down, 0.0)
        own.append(here + jnp.where(lane < pixels - width, up, 0.0))
        edge.append(jnp.where(lane < width, down, up))
    return jnp.concatenate(own, axis=1), jnp.concatenate(edge, axis=1)


def tokens_part(latent, noise, pick, flow_t, chans):
    tokens = pick.shape[1] // 4
    terms = split(latent, 3) + split(noise, 3)
    moved = dot(jnp.concatenate(terms, axis=0), pick)
    lat = moved[:chans] + moved[chans : 2 * chans] + moved[2 * chans : 3 * chans]
    noi = moved[3 * chans : 4 * chans] + moved[4 * chans : 5 * chans] + moved[5 * chans :]
    noisy = (1.0 - flow_t) * lat + flow_t * noi
    velocity = noi - lat
    stacked = jnp.concatenate(
        [noisy[:, k * tokens : (k + 1) * tokens] for k in range(4)]
        + [velocity[:, k * tokens : (k + 1) * tokens] for k in range(4)],
        axis=0,
    )
    flipped = stacked.T
    return flipped[:, : 4 * chans], flipped[:, 4 * chans :]


def norm_part(noisy, velocity, embed_ref, time_rows, chunk):
    tokens, patch = noisy.shape
    depth = embed_ref.shape[1]
    lhs = jnp.concatenate(
        [jnp.concatenate(split(noisy, 3), axis=1), jnp.concatenate(split(velocity, 3), axis=1)], axis=0
    )
    square = jnp.zeros((tokens, chunk), F32)
    cross = jnp.zeros((tokens, chunk), F32)
    for k in range(depth // chunk):
        piece = embed_ref[:, k * chunk : (k + 1) * chunk]
        both = dot(lhs, jnp.concatenate([piece, piece, piece], axis=0))
        hidden = both[:tokens] + time_rows[0:1, k * chunk : (k + 1) * chunk]
        hidden_t = both[tokens:] + time_rows[1:2, k * chunk : (k + 1) * chunk]
        square = square + hidden * hidden
        cross = cross + hidden * hidden_t
    mean_sq = jnp.sum(square, axis=1, keepdims=True) / depth
    mean_cr = jnp.sum(cross, axis=1, keepdims=True) / depth
    inv = lax.rsqrt(mean_sq + EPSILON)
    shift = -(inv * inv * inv) * mean_cr
    inv_hi, inv_lo = [v.astype(F32) for v in split(inv, 2)]
    sh_hi, sh_lo = [v.astype(F32) for v in split(shift, 2)]
    lane = lax.broadcasted_iota(jnp.int32, (tokens, LANES - patch), 1)

    def tail(*columns):
        out = jnp.zeros((tokens, LANES - patch), F32)
        for index, column in enumerate(columns):
            out = jnp.where(lane == index, column, out)
        return out

    rows = jnp.concatenate([noisy * inv, tail(inv_hi, inv_lo, inv_hi)], axis=1)
    rows_t = jnp.concatenate(
        [velocity * inv + noisy * shift, tail(sh_hi, sh_lo, sh_hi, inv_hi, inv_lo, inv_hi)], axis=1
    )
    return rows.astype(BF16), rows_t.astype(BF16)


MESH = pl.DeviceIdType.MESH


def front_kernel(
    dims,
    flow_ref, source_ref, w_hbm, ecut_hbm, gcut_hbm, tcut_hbm, f_hbm, enc_hbm, time_hbm, noise_hbm, embed_hbm,
    x_out, x_own, m_out,
    w_ref, ecut_ref, gcut_ref, tcut_ref, f_ref, enc_ref, time_ref, noise_ref, embed_ref, load_sem, feats_ref,
    feats_buf, feats_send, feats_recv,
    edge_buf, before_buf, after_buf, edge_send, edge_recv,
    e_send, e_recv, tau_send, tau_recv, e_ss, e_rs, t_ss, t_rs,
    x_buf, x_ss, x_rs,
    g_buf, tau_buf, b_ss, b_rs, bt_ss, bt_rs, a_ss, a_rs, c_ss, c_rs,
):
    frames, width, chans, peers, clips = dims
    seq, clip = lax.axis_index("seq"), lax.axis_index("clip")
    patch, depth = embed_ref.shape
    share = ecut_ref.shape[1]
    part = w_ref.shape[2]
    chunk = patch // clips
    on_seq = [{"seq": lax.rem(seq + k, peers)} for k in range(1, peers)]
    on_clip = [{"clip": lax.rem(clip + k, clips)} for k in range(1, clips)]
    mate = {"clip": clip + 1 - 2 * lax.rem(clip, 2)}

    def cut(ref):
        if ref.shape[-1] == share:
            return ref
        return ref.at[:, pl.ds(pl.multiple_of(clip * share, share), share)]

    pairs = (
        (w_hbm, w_ref), (cut(ecut_hbm), ecut_ref), (cut(gcut_hbm), gcut_ref), (cut(tcut_hbm), tcut_ref),
        (f_hbm, f_ref), (enc_hbm, enc_ref), (time_hbm, time_ref), (noise_hbm, noise_ref), (embed_hbm, embed_ref),
    )
    loads = [pltpu.make_async_copy(src, dst, load_sem.at[k]) for k, (src, dst) in enumerate(pairs)]
    for load in loads:
        load.start()
    flow_r = flow_ref[0, 0].astype(F32) / TGRID
    flow_t = flow_ref[0, 1].astype(F32) / TGRID
    quarter = TFEAT // 4
    order = lax.broadcasted_iota(jnp.int32, (8, TFEAT), 1)
    line = lax.broadcasted_iota(jnp.int32, (8, TFEAT), 0)
    omega = 8.0 * jnp.exp(-np.float32(np.log(100.0)) * lax.rem(order, quarter).astype(F32) / quarter)
    angle = omega * jnp.where(order < 2 * quarter, flow_t, flow_t - flow_r)
    sine, cosine = jnp.sin(angle), jnp.cos(angle)
    first = lax.rem(order // quarter, 2) == 0
    feats_ref[...] = jnp.where(
        line == 0,
        jnp.where(first, sine, cosine),
        jnp.where(line == 1, jnp.where(first, omega * cosine, -omega * sine), 0.0),
    )

    barrier = pltpu.get_barrier_semaphore()
    for who in on_seq + on_clip:
        pl.semaphore_signal(barrier, inc=1, device_id=who, device_id_type=MESH)
    pl.semaphore_wait(barrier, len(on_seq) + len(on_clip))
    sent = []

    def push(src, dst, ssem, rsem, who):
        copy = pltpu.make_async_remote_copy(
            src_ref=src, dst_ref=dst, send_sem=ssem, recv_sem=rsem, device_id=who, device_id_type=MESH
        )
        copy.start()
        sent.append(copy)
        return copy

    feats_in = [
        push(feats_ref, feats_buf.at[clip], feats_send.at[k], feats_recv.at[k], who) for k, who in enumerate(on_clip)
    ]
    feats_buf[clip] = feats_ref[...]

    loads[1].wait()
    loads[2].wait()
    gain = gcut_ref[...]
    left = jnp.concatenate(split(ecut_ref[...].astype(F32) * gain, 2), axis=0)
    loads[0].wait()
    for i in range(3):
        both = dot(left, w_ref[i])
        both = both[:patch] + both[patch:]
        for c in range(clips):
            e_send[c, :, i * part : (i + 1) * part] = both[c * chunk : (c + 1) * chunk]
    e_in = [
        push(e_send.at[lax.rem(clip + k + 1, clips)], e_recv.at[k], e_ss.at[k], e_rs.at[k], who)
        for k, who in enumerate(on_clip)
    ]
    for copy in feats_in:
        copy.wait_recv()
    loads[3].wait()
    feats = feats_buf[...].reshape(clips * 8, feats_buf.shape[2])
    both = dot(jnp.concatenate(split(feats, 2), axis=0), tcut_ref[...])
    left = jnp.concatenate(split((both[: clips * 8] + both[clips * 8 :]) * gain, 2), axis=0)
    for i in range(3):
        both = dot(left, w_ref[i])
        both = both[: clips * 8] + both[clips * 8 :]
        for c in range(clips):
            tau_send[c, :, i * part : (i + 1) * part] = both[c * 8 : c * 8 + 2]
    tau_in = [
        push(tau_send.at[lax.rem(clip + k + 1, clips)], tau_recv.at[k], t_ss.at[k], t_rs.at[k], who)
        for k, who in enumerate(on_clip)
    ]

    loads[4].wait()
    loads[5].wait()
    own, edge = conv_part(f_ref, enc_ref, frames, width, chans)
    edge_buf[...] = edge

    def edge_copy(dst, k, step):
        return pltpu.make_async_remote_copy(
            src_ref=edge_buf, dst_ref=dst, send_sem=edge_send.at[k], recv_sem=edge_recv.at[k],
            device_id={"seq": lax.rem(seq + peers + step, peers)}, device_id_type=MESH,
        )

    to_next, to_last = edge_copy(before_buf, 0, 1), edge_copy(after_buf, 1, -1)

    @pl.when(seq < peers - 1)
    def _():
        to_next.start()

    @pl.when(seq > 0)
    def _():
        to_last.start()

    @pl.when(seq == 0)
    def _():
        before_buf[...] = jnp.zeros_like(before_buf)

    @pl.when(seq == peers - 1)
    def _():
        after_buf[...] = jnp.zeros_like(after_buf)

    loads[6].wait()
    mine = jnp.concatenate(split(feats_ref[...], 2), axis=0)
    times = dot(mine, time_ref[...])
    times = times[:8] + times[8:]

    for copy in e_in:
        copy.wait_recv()
    total = e_send[clip]
    for k in range(clips - 1):
        total = total + e_recv[k]
    g_buf[clip, seq] = total.astype(BF16)
    b_in = [
        push(g_buf.at[clip, seq], g_buf.at[clip, seq], b_ss.at[k], b_rs.at[k], who) for k, who in enumerate(on_seq)
    ]
    for copy in tau_in:
        copy.wait_recv()
    total = tau_send[clip]
    for k in range(clips - 1):
        total = total + tau_recv[k]
    tau_buf[seq] = total
    bt_in = [
        push(tau_buf.at[seq], tau_buf.at[seq], bt_ss.at[k], bt_rs.at[k], who) for k, who in enumerate(on_seq)
    ]
    @pl.when(seq > 0)
    def _():
        to_next.wait_recv()

    @pl.when(seq < peers - 1)
    def _():
        to_last.wait_recv()

    pixels = f_ref.shape[1]
    lane = lax.rem(lax.broadcasted_iota(jnp.int32, own.shape, 1), pixels)
    latent = own + jnp.where(lane < width, before_buf[...], 0.0)
    latent = latent + jnp.where(lane >= pixels - width, after_buf[...], 0.0)
    loads[7].wait()
    loads[8].wait()
    noise = jnp.concatenate(
        [noise_ref[f, r] for f in range(frames) for r in range(noise_ref.shape[1])], axis=1
    )
    places = lax.broadcasted_iota(jnp.int32, (own.shape[1], source_ref.shape[1]), 0)
    pick = (places == source_ref[...]).astype(F32).astype(BF16)
    noisy, velocity = tokens_part(latent, noise, pick, flow_t, chans)
    rows, rows_t = norm_part(noisy, velocity, embed_ref, times, 512)
    x_buf[seq, 0] = rows
    x_buf[seq, 1] = rows_t
    x_in = [push(x_buf.at[seq], x_buf.at[seq], x_ss.at[k], x_rs.at[k], who) for k, who in enumerate(on_seq)]

    for copy in b_in:
        copy.wait_recv()
    c_in = [push(g_buf.at[clip], g_buf.at[clip], c_ss.at[0], c_rs.at[0], mate)]
    a_in = [
        push(g_buf.at[clip], g_buf.at[clip], a_ss.at[k], a_rs.at[k], on_clip[2 * k + 1])
        for k in range(clips // 2 - 1)
    ]
    for k, copy in enumerate(a_in):
        copy.wait_recv()
        src = lax.rem(clip + clips - 2 * (k + 1), clips)
        c_in.append(push(g_buf.at[src], g_buf.at[src], c_ss.at[k + 1], c_rs.at[k + 1], mate))
    for copy in bt_in + x_in + c_in:
        copy.wait_recv()
    tokens = x_buf.shape[2]
    x_own[:tokens] = x_buf[seq, 0]
    x_own[tokens:] = x_buf[seq, 1]
    for p in range(peers):
        x_out[p * tokens : (p + 1) * tokens] = x_buf[p, 0]
        x_out[(peers + p) * tokens : (peers + p + 1) * tokens] = x_buf[p, 1]
        for c in range(clips):
            m_out[p, c * chunk : (c + 1) * chunk] = g_buf[c, p]
        hi = tau_buf[p].astype(BF16).astype(F32)
        lo = tau_buf[p] - hi
        extra = [hi[0:1], hi[0:1], lo[0:1], hi[1:2], hi[1:2], lo[1:2]]
        row = lax.broadcasted_iota(jnp.int32, (LANES - patch, 3 * part), 0)
        tail = jnp.zeros((LANES - patch, 3 * part), F32)
        for index, value in enumerate(extra):
            tail = jnp.where(row == index, value, tail)
        m_out[p, patch:] = tail.astype(BF16)
    for copy in sent:
        copy.wait_send()

    @pl.when(seq < peers - 1)
    def _():
        to_next.wait_send()

    @pl.when(seq > 0)
    def _():
        to_last.wait_send()


def attend_kernel(per, x_ref, own_ref, q_ref, k_ref, v_ref, out_ref, out_t_ref):
    scale = HD ** (-0.5)
    total, tokens = x_ref.shape[0] // 2, own_ref.shape[0] // 2
    keys = dot(x_ref[...], k_ref[0]).astype(BF16)
    vals = dot(x_ref[...], v_ref[0]).astype(BF16)
    query = dot(own_ref[...], q_ref[0]).astype(BF16)
    zero = jnp.zeros((tokens, HD), BF16)
    for h in range(per):
        at = slice(h * HD, (h + 1) * HD)
        q, qt = query[:tokens, at], query[tokens:, at]
        left = jnp.concatenate(
            [jnp.concatenate([q, zero], axis=1), jnp.concatenate([qt, q], axis=1)], axis=0
        )
        both = dot_nt(left, jnp.concatenate([keys[:total, at], keys[total:, at]], axis=1))
        scores, score_t = both[:tokens], both[tokens:]
        expo = jnp.exp((scores - jnp.max(scores, axis=1, keepdims=True)) * scale)
        inv = 1.0 / jnp.sum(expo, axis=1, keepdims=True)
        mean = jnp.sum(expo * score_t, axis=1, keepdims=True) * inv
        left = jnp.concatenate([expo.astype(BF16), (expo * (score_t - mean)).astype(BF16)], axis=0)
        both = dot(left, jnp.concatenate([vals[:total, at], vals[total:, at]], axis=1))
        out_ref[:, at] = (both[:tokens, :HD] * inv).astype(BF16)
        out_t_ref[:, at] = (both[tokens:, :HD] * (inv * scale) + both[:tokens, HD:] * inv).astype(BF16)


VMEM = pl.BlockSpec(memory_space=pltpu.VMEM)


def attend(rows, own, weights, inner):
    peers, depth, width = weights.shape
    part = width // 3
    per = part // HD
    block = per * HD
    count = part // block
    tokens, total = own.shape[0] // 2, rows.shape[0]
    whole = lambda n: pl.BlockSpec((n, LANES), lambda i: (0, 0))
    spec = lambda g: pl.BlockSpec((1, depth, block), lambda i: (i // count, 0, g * count + i % count))
    out = pl.BlockSpec((tokens, block), lambda i: (0, i))
    shape = jax.ShapeDtypeStruct((tokens, inner), BF16)
    return pl.pallas_call(
        functools.partial(attend_kernel, per),
        grid=(peers * count,),
        out_shape=(shape, shape),
        in_specs=[whole(total), whole(2 * tokens), spec(0), spec(1), spec(2)],
        out_specs=(out, out),
        name="attend",
    )(rows, own, weights, weights, weights)


def local(clip_features, enc_weight, noise_field, flow_times, embed_weight, time_weight, norm_gain, qkv_weight):
    _, frames, rows, width, depth_c = clip_features.shape
    chans = enc_weight.shape[4]
    patch, depth = embed_weight.shape
    peers, clips = lax.axis_size("seq"), lax.axis_size("clip")
    share = qkv_weight.shape[0]
    part = qkv_weight.shape[2]
    pixels = rows * width
    tokens = frames * pixels // 4

    gain, embed_cut, time_cut = norm_gain[None, :], embed_weight, time_weight
    if share % LANES:
        me = lax.axis_index("clip")
        gain, embed_cut, time_cut = (
            lax.dynamic_slice_in_dim(m, me * share, share, 1) for m in (gain, embed_weight, time_weight)
        )
    weight = qkv_weight.transpose(1, 0, 2)
    features = clip_features.reshape(frames, pixels, depth_c)
    enc = enc_weight.transpose(0, 1, 2, 4, 3).reshape(27 * chans, depth_c)
    noise = noise_field[0].transpose(0, 1, 3, 2)
    i, f, j = np.meshgrid(np.arange(rows // 2), np.arange(frames), np.arange(width // 2), indexing="ij")
    source = np.stack(
        [((f * rows + 2 * i + p) * width + 2 * j + q).reshape(-1) for p in range(2) for q in range(2)]
    ).reshape(1, -1)
    source = jnp.asarray(source.astype(np.int32))
    chunk = patch // clips
    dma = pltpu.SemaphoreType.DMA
    anywhere = pl.BlockSpec(memory_space=pl.ANY)
    edge = pltpu.VMEM((chans, frames * pixels), F32)
    x, x_own, weights = pl.pallas_call(
        functools.partial(front_kernel, (frames, width, chans, peers, clips)),
        out_shape=(
            jax.ShapeDtypeStruct((2 * peers * tokens, LANES), BF16),
            jax.ShapeDtypeStruct((2 * tokens, LANES), BF16),
            jax.ShapeDtypeStruct((peers, LANES, 3 * part), BF16),
        ),
        in_specs=[pl.BlockSpec(memory_space=pltpu.SMEM), VMEM] + [anywhere] * 9,
        out_specs=(VMEM,) * 3,
        scratch_shapes=[
            pltpu.VMEM(weight.shape, BF16), pltpu.VMEM((patch, share), BF16), pltpu.VMEM((1, share), F32),
            pltpu.VMEM((TFEAT, share), BF16), pltpu.VMEM(features.shape, BF16), pltpu.VMEM(enc.shape, BF16),
            pltpu.VMEM(time_weight.shape, BF16), pltpu.VMEM(noise.shape, F32), pltpu.VMEM(embed_weight.shape, BF16),
            dma((9,)), pltpu.VMEM((8, TFEAT), F32),
            pltpu.VMEM((clips, 8, TFEAT), F32), dma((clips - 1,)), dma((clips - 1,)),
            edge, edge, edge, dma((2,)), dma((2,)),
            pltpu.VMEM((clips, chunk, 3 * part), F32), pltpu.VMEM((clips - 1, chunk, 3 * part), F32),
            pltpu.VMEM((clips, 2, 3 * part), F32), pltpu.VMEM((clips - 1, 2, 3 * part), F32),
            dma((clips - 1,)), dma((clips - 1,)), dma((clips - 1,)), dma((clips - 1,)),
            pltpu.VMEM((peers, 2, tokens, LANES), BF16), dma((peers - 1,)), dma((peers - 1,)),
            pltpu.VMEM((clips, peers, chunk, 3 * part), BF16), pltpu.VMEM((peers, 2, 3 * part), F32),
            dma((peers - 1,)), dma((peers - 1,)), dma((peers - 1,)), dma((peers - 1,)),
            dma((clips // 2,)), dma((clips // 2,)), dma((clips // 2,)), dma((clips // 2,)),
        ],
        compiler_params=pltpu.CompilerParams(collective_id=0, has_side_effects=True),
        name="front",
    )(flow_times, source, weight, embed_cut, gain, time_cut, features, enc, time_weight, noise, embed_weight)
    output, output_t = attend(x, x_own, weights, peers * part)
    return output[None], output_t[None]


def solution(mesh):
    placed = (
        P("clip", None, "seq", None, None),
        P(),
        P("clip", None, "seq", None, None),
        P("clip", None),
        P(),
        P(),
        P(),
        P("clip", None, "seq"),
    )
    return jax.shard_map(
        local,
        mesh=mesh,
        in_specs=placed,
        out_specs=(P("clip", "seq", None), P("clip", "seq", None)),
        check_vma=False,
    )
```

```python
import functools

import jax
import jax.numpy as jnp
import numpy as np
from jax import lax
from jax.experimental import pallas as pl
from jax.experimental.pallas import tpu as pltpu
from jax.sharding import PartitionSpec as P

HD = 128
TFEAT = 256
TGRID = 1000
EPSILON = 1e-06
LANES = 128
F32 = jnp.float32
BF16 = jnp.bfloat16


def split(value, parts):
    terms = []
    for _ in range(parts):
        term = value.astype(BF16)
        terms.append(term)
        value = value - term.astype(F32)
    return terms


def dot(a, b):
    return jnp.dot(a, b, preferred_element_type=F32)


def dot_nt(a, b):
    return lax.dot_general(a, b, (((1,), (1,)), ((), ())), preferred_element_type=F32)


def conv_part(features, weight, frames, width, chans):
    pixels = features.shape[1]
    taps = [dot_nt(weight[...], features[f]) for f in range(frames)]
    lane = lax.broadcasted_iota(jnp.int32, (chans, pixels), 1)
    column = lax.rem(lane, width)
    block = 9 * chans
    own, edge = [], []
    for f in range(frames):
        acc = taps[f][2 * block : 3 * block]
        if f >= 1:
            acc = acc + taps[f - 1][block : 2 * block]
        if f >= 2:
            acc = acc + taps[f - 2][:block]
        rows = []
        for b in range(3):
            part = [acc[(b * 3 + e) * chans : (b * 3 + e + 1) * chans] for e in range(3)]
            total = part[1]
            total = total + jnp.where(column > 0, pltpu.roll(part[0], 1, 1), 0.0)
            total = total + jnp.where(column < width - 1, pltpu.roll(part[2], pixels - 1, 1), 0.0)
            rows.append(total)
        down = pltpu.roll(rows[0], width, 1)
        up = pltpu.roll(rows[2], pixels - width, 1)
        here = rows[1] + jnp.where(lane >= width, down, 0.0)
        own.append(here + jnp.where(lane < pixels - width, up, 0.0))
        edge.append(jnp.where(lane < width, down, up))
    return jnp.concatenate(own, axis=1), jnp.concatenate(edge, axis=1)


def tokens_part(latent, noise, pick, flow_t, chans):
    tokens = pick.shape[1] // 4
    terms = split(latent, 3) + split(noise, 3)
    moved = dot(jnp.concatenate(terms, axis=0), pick)
    lat = moved[:chans] + moved[chans : 2 * chans] + moved[2 * chans : 3 * chans]
    noi = moved[3 * chans : 4 * chans] + moved[4 * chans : 5 * chans] + moved[5 * chans :]
    noisy = (1.0 - flow_t) * lat + flow_t * noi
    velocity = noi - lat
    stacked = jnp.concatenate(
        [noisy[:, k * tokens : (k + 1) * tokens] for k in range(4)]
        + [velocity[:, k * tokens : (k + 1) * tokens] for k in range(4)],
        axis=0,
    )
    flipped = stacked.T
    return flipped[:, : 4 * chans], flipped[:, 4 * chans :]


def norm_part(noisy, velocity, embed_ref, time_rows, chunk):
    tokens, patch = noisy.shape
    depth = embed_ref.shape[1]
    lhs = jnp.concatenate(
        [jnp.concatenate(split(noisy, 3), axis=1), jnp.concatenate(split(velocity, 3), axis=1)], axis=0
    )
    square = jnp.zeros((tokens, chunk), F32)
    cross = jnp.zeros((tokens, chunk), F32)
    for k in range(depth // chunk):
        piece = embed_ref[:, k * chunk : (k + 1) * chunk]
        both = dot(lhs, jnp.concatenate([piece, piece, piece], axis=0))
        hidden = both[:tokens] + time_rows[0:1, k * chunk : (k + 1) * chunk]
        hidden_t = both[tokens:] + time_rows[1:2, k * chunk : (k + 1) * chunk]
        square = square + hidden * hidden
        cross = cross + hidden * hidden_t
    mean_sq = jnp.sum(square, axis=1, keepdims=True) / depth
    mean_cr = jnp.sum(cross, axis=1, keepdims=True) / depth
    inv = lax.rsqrt(mean_sq + EPSILON)
    shift = -(inv * inv * inv) * mean_cr
    inv_hi, inv_lo = [v.astype(F32) for v in split(inv, 2)]
    sh_hi, sh_lo = [v.astype(F32) for v in split(shift, 2)]
    lane = lax.broadcasted_iota(jnp.int32, (tokens, LANES - patch), 1)

    def tail(*columns):
        out = jnp.zeros((tokens, LANES - patch), F32)
        for index, column in enumerate(columns):
            out = jnp.where(lane == index, column, out)
        return out

    rows = jnp.concatenate([noisy * inv, tail(inv_hi, inv_lo, inv_hi)], axis=1)
    rows_t = jnp.concatenate(
        [velocity * inv + noisy * shift, tail(sh_hi, sh_lo, sh_hi, inv_hi, inv_lo, inv_hi)], axis=1
    )
    return rows.astype(BF16), rows_t.astype(BF16)


MESH = pl.DeviceIdType.MESH


def front_kernel(
    dims,
    flow_ref, source_ref, w_hbm, ecut_hbm, gcut_hbm, tcut_hbm, f_hbm, enc_hbm, time_hbm, noise_hbm, embed_hbm,
    x_out, x_own, m_out,
    w_ref, ecut_ref, gcut_ref, tcut_ref, f_ref, enc_ref, time_ref, noise_ref, embed_ref, load_sem, feats_ref,
    feats_buf, feats_send, feats_recv,
    edge_buf, before_buf, after_buf, edge_send, edge_recv,
    e_send, e_recv, tau_send, tau_recv, e_ss, e_rs, t_ss, t_rs,
    x_buf, x_ss, x_rs,
    g_buf, tau_buf, b_ss, b_rs, bt_ss, bt_rs, a_ss, a_rs, c_ss, c_rs,
):
    frames, width, chans, peers, clips = dims
    seq, clip = lax.axis_index("seq"), lax.axis_index("clip")
    patch, depth = embed_ref.shape
    share = ecut_ref.shape[1]
    part = w_ref.shape[2]
    chunk = patch // clips
    on_seq = [{"seq": lax.rem(seq + k, peers)} for k in range(1, peers)]
    on_clip = [{"clip": lax.rem(clip + k, clips)} for k in range(1, clips)]
    mate = {"clip": clip + 1 - 2 * lax.rem(clip, 2)}

    def cut(ref):
        if ref.shape[-1] == share:
            return ref
        return ref.at[:, pl.ds(pl.multiple_of(clip * share, share), share)]

    pairs = (
        (w_hbm, w_ref), (cut(ecut_hbm), ecut_ref), (cut(gcut_hbm), gcut_ref), (cut(tcut_hbm), tcut_ref),
        (f_hbm, f_ref), (enc_hbm, enc_ref), (time_hbm, time_ref), (noise_hbm, noise_ref), (embed_hbm, embed_ref),
    )
    loads = [pltpu.make_async_copy(src, dst, load_sem.at[k]) for k, (src, dst) in enumerate(pairs)]
    for load in loads:
        load.start()
    flow_r = flow_ref[0, 0].astype(F32) / TGRID
    flow_t = flow_ref[0, 1].astype(F32) / TGRID
    quarter = TFEAT // 4
    order = lax.broadcasted_iota(jnp.int32, (8, TFEAT), 1)
    line = lax.broadcasted_iota(jnp.int32, (8, TFEAT), 0)
    omega = 8.0 * jnp.exp(-np.float32(np.log(100.0)) * lax.rem(order, quarter).astype(F32) / quarter)
    angle = omega * jnp.where(order < 2 * quarter, flow_t, flow_t - flow_r)
    sine, cosine = jnp.sin(angle), jnp.cos(angle)
    first = lax.rem(order // quarter, 2) == 0
    feats_ref[...] = jnp.where(
        line == 0,
        jnp.where(first, sine, cosine),
        jnp.where(line == 1, jnp.where(first, omega * cosine, -omega * sine), 0.0),
    )

    barrier = pltpu.get_barrier_semaphore()
    for who in on_seq + on_clip:
        pl.semaphore_signal(barrier, inc=1, device_id=who, device_id_type=MESH)
    pl.semaphore_wait(barrier, len(on_seq) + len(on_clip))
    sent = []

    def push(src, dst, ssem, rsem, who):
        copy = pltpu.make_async_remote_copy(
            src_ref=src, dst_ref=dst, send_sem=ssem, recv_sem=rsem, device_id=who, device_id_type=MESH
        )
        copy.start()
        sent.append(copy)
        return copy

    feats_in = [
        push(feats_ref, feats_buf.at[clip], feats_send.at[k], feats_recv.at[k], who) for k, who in enumerate(on_clip)
    ]
    feats_buf[clip] = feats_ref[...]

    loads[1].wait()
    loads[2].wait()
    gain = gcut_ref[...]
    left = jnp.concatenate(split(ecut_ref[...].astype(F32) * gain, 2), axis=0)
    loads[0].wait()
    for i in range(3):
        both = dot(left, w_ref[i])
        both = both[:patch] + both[patch:]
        for c in range(clips):
            e_send[c, :, i * part : (i + 1) * part] = both[c * chunk : (c + 1) * chunk].astype(BF16)
    e_in = [
        push(e_send.at[lax.rem(clip + k + 1, clips)], e_recv.at[k], e_ss.at[k], e_rs.at[k], who)
        for k, who in enumerate(on_clip)
    ]
    for copy in feats_in:
        copy.wait_recv()
    loads[3].wait()
    feats = feats_buf[...].reshape(clips * 8, feats_buf.shape[2])
    both = dot(jnp.concatenate(split(feats, 2), axis=0), tcut_ref[...])
    left = jnp.concatenate(split((both[: clips * 8] + both[clips * 8 :]) * gain, 2), axis=0)
    for i in range(3):
        both = dot(left, w_ref[i])
        both = both[: clips * 8] + both[clips * 8 :]
        for c in range(clips):
            tau_send[c, :, i * part : (i + 1) * part] = both[c * 8 : c * 8 + 2]
    tau_in = [
        push(tau_send.at[lax.rem(clip + k + 1, clips)], tau_recv.at[k], t_ss.at[k], t_rs.at[k], who)
        for k, who in enumerate(on_clip)
    ]

    loads[4].wait()
    loads[5].wait()
    own, edge = conv_part(f_ref, enc_ref, frames, width, chans)
    edge_buf[...] = edge

    def edge_copy(dst, k, step):
        return pltpu.make_async_remote_copy(
            src_ref=edge_buf, dst_ref=dst, send_sem=edge_send.at[k], recv_sem=edge_recv.at[k],
            device_id={"seq": lax.rem(seq + peers + step, peers)}, device_id_type=MESH,
        )

    to_next, to_last = edge_copy(before_buf, 0, 1), edge_copy(after_buf, 1, -1)

    @pl.when(seq < peers - 1)
    def _():
        to_next.start()

    @pl.when(seq > 0)
    def _():
        to_last.start()

    @pl.when(seq == 0)
    def _():
        before_buf[...] = jnp.zeros_like(before_buf)

    @pl.when(seq == peers - 1)
    def _():
        after_buf[...] = jnp.zeros_like(after_buf)

    loads[6].wait()
    mine = jnp.concatenate(split(feats_ref[...], 2), axis=0)
    times = dot(mine, time_ref[...])
    times = times[:8] + times[8:]

    for copy in e_in:
        copy.wait_recv()
    total = e_send[clip].astype(F32)
    for k in range(clips - 1):
        total = total + e_recv[k].astype(F32)
    g_buf[clip, seq] = total.astype(BF16)
    b_in = [
        push(g_buf.at[clip, seq], g_buf.at[clip, seq], b_ss.at[k], b_rs.at[k], who) for k, who in enumerate(on_seq)
    ]
    for copy in tau_in:
        copy.wait_recv()
    total = tau_send[clip]
    for k in range(clips - 1):
        total = total + tau_recv[k]
    tau_buf[seq] = total
    bt_in = [
        push(tau_buf.at[seq], tau_buf.at[seq], bt_ss.at[k], bt_rs.at[k], who) for k, who in enumerate(on_seq)
    ]
    @pl.when(seq > 0)
    def _():
        to_next.wait_recv()

    @pl.when(seq < peers - 1)
    def _():
        to_last.wait_recv()

    pixels = f_ref.shape[1]
    lane = lax.rem(lax.broadcasted_iota(jnp.int32, own.shape, 1), pixels)
    latent = own + jnp.where(lane < width, before_buf[...], 0.0)
    latent = latent + jnp.where(lane >= pixels - width, after_buf[...], 0.0)
    loads[7].wait()
    loads[8].wait()
    noise = jnp.concatenate(
        [noise_ref[f, r] for f in range(frames) for r in range(noise_ref.shape[1])], axis=1
    )
    places = lax.broadcasted_iota(jnp.int32, (own.shape[1], source_ref.shape[1]), 0)
    pick = (places == source_ref[...]).astype(F32).astype(BF16)
    noisy, velocity = tokens_part(latent, noise, pick, flow_t, chans)
    rows, rows_t = norm_part(noisy, velocity, embed_ref, times, 512)
    x_buf[seq, 0] = rows
    x_buf[seq, 1] = rows_t
    x_in = [push(x_buf.at[seq], x_buf.at[seq], x_ss.at[k], x_rs.at[k], who) for k, who in enumerate(on_seq)]

    for copy in b_in:
        copy.wait_recv()
    c_in = [push(g_buf.at[clip], g_buf.at[clip], c_ss.at[0], c_rs.at[0], mate)]
    a_in = [
        push(g_buf.at[clip], g_buf.at[clip], a_ss.at[k], a_rs.at[k], on_clip[2 * k + 1])
        for k in range(clips // 2 - 1)
    ]
    for k, copy in enumerate(a_in):
        copy.wait_recv()
        src = lax.rem(clip + clips - 2 * (k + 1), clips)
        c_in.append(push(g_buf.at[src], g_buf.at[src], c_ss.at[k + 1], c_rs.at[k + 1], mate))
    for copy in bt_in + x_in + c_in:
        copy.wait_recv()
    tokens = x_buf.shape[2]
    x_own[:tokens] = x_buf[seq, 0]
    x_own[tokens:] = x_buf[seq, 1]
    for p in range(peers):
        x_out[p * tokens : (p + 1) * tokens] = x_buf[p, 0]
        x_out[(peers + p) * tokens : (peers + p + 1) * tokens] = x_buf[p, 1]
        for c in range(clips):
            m_out[p, c * chunk : (c + 1) * chunk] = g_buf[c, p]
        hi = tau_buf[p].astype(BF16).astype(F32)
        lo = tau_buf[p] - hi
        extra = [hi[0:1], hi[0:1], lo[0:1], hi[1:2], hi[1:2], lo[1:2]]
        row = lax.broadcasted_iota(jnp.int32, (LANES - patch, 3 * part), 0)
        tail = jnp.zeros((LANES - patch, 3 * part), F32)
        for index, value in enumerate(extra):
            tail = jnp.where(row == index, value, tail)
        m_out[p, patch:] = tail.astype(BF16)
    for copy in sent:
        copy.wait_send()

    @pl.when(seq < peers - 1)
    def _():
        to_next.wait_send()

    @pl.when(seq > 0)
    def _():
        to_last.wait_send()


def attend_kernel(per, x_ref, own_ref, q_ref, k_ref, v_ref, out_ref, out_t_ref):
    scale = HD ** (-0.5)
    total, tokens = x_ref.shape[0] // 2, own_ref.shape[0] // 2
    keys = dot(x_ref[...], k_ref[0]).astype(BF16)
    vals = dot(x_ref[...], v_ref[0]).astype(BF16)
    query = dot(own_ref[...], q_ref[0]).astype(BF16)
    zero = jnp.zeros((tokens, HD), BF16)
    for h in range(per):
        at = slice(h * HD, (h + 1) * HD)
        q, qt = query[:tokens, at], query[tokens:, at]
        left = jnp.concatenate(
            [jnp.concatenate([q, zero], axis=1), jnp.concatenate([qt, q], axis=1)], axis=0
        )
        both = dot_nt(left, jnp.concatenate([keys[:total, at], keys[total:, at]], axis=1))
        scores, score_t = both[:tokens], both[tokens:]
        expo = jnp.exp((scores - jnp.max(scores, axis=1, keepdims=True)) * scale)
        inv = 1.0 / jnp.sum(expo, axis=1, keepdims=True)
        mean = jnp.sum(expo * score_t, axis=1, keepdims=True) * inv
        left = jnp.concatenate([expo.astype(BF16), (expo * (score_t - mean)).astype(BF16)], axis=0)
        both = dot(left, jnp.concatenate([vals[:total, at], vals[total:, at]], axis=1))
        out_ref[:, at] = (both[:tokens, :HD] * inv).astype(BF16)
        out_t_ref[:, at] = (both[tokens:, :HD] * (inv * scale) + both[:tokens, HD:] * inv).astype(BF16)


VMEM = pl.BlockSpec(memory_space=pltpu.VMEM)


def attend(rows, own, weights, inner):
    peers, depth, width = weights.shape
    part = width // 3
    per = part // HD
    block = per * HD
    count = part // block
    tokens, total = own.shape[0] // 2, rows.shape[0]
    whole = lambda n: pl.BlockSpec((n, LANES), lambda i: (0, 0))
    spec = lambda g: pl.BlockSpec((1, depth, block), lambda i: (i // count, 0, g * count + i % count))
    out = pl.BlockSpec((tokens, block), lambda i: (0, i))
    shape = jax.ShapeDtypeStruct((tokens, inner), BF16)
    return pl.pallas_call(
        functools.partial(attend_kernel, per),
        grid=(peers * count,),
        out_shape=(shape, shape),
        in_specs=[whole(total), whole(2 * tokens), spec(0), spec(1), spec(2)],
        out_specs=(out, out),
        name="attend",
    )(rows, own, weights, weights, weights)


def local(clip_features, enc_weight, noise_field, flow_times, embed_weight, time_weight, norm_gain, qkv_weight):
    _, frames, rows, width, depth_c = clip_features.shape
    chans = enc_weight.shape[4]
    patch, depth = embed_weight.shape
    peers, clips = lax.axis_size("seq"), lax.axis_size("clip")
    share = qkv_weight.shape[0]
    part = qkv_weight.shape[2]
    pixels = rows * width
    tokens = frames * pixels // 4

    gain, embed_cut, time_cut = norm_gain[None, :], embed_weight, time_weight
    if share % LANES:
        me = lax.axis_index("clip")
        gain, embed_cut, time_cut = (
            lax.dynamic_slice_in_dim(m, me * share, share, 1) for m in (gain, embed_weight, time_weight)
        )
    weight = qkv_weight.transpose(1, 0, 2)
    features = clip_features.reshape(frames, pixels, depth_c)
    enc = enc_weight.transpose(0, 1, 2, 4, 3).reshape(27 * chans, depth_c)
    noise = noise_field[0].transpose(0, 1, 3, 2)
    i, f, j = np.meshgrid(np.arange(rows // 2), np.arange(frames), np.arange(width // 2), indexing="ij")
    source = np.stack(
        [((f * rows + 2 * i + p) * width + 2 * j + q).reshape(-1) for p in range(2) for q in range(2)]
    ).reshape(1, -1)
    source = jnp.asarray(source.astype(np.int32))
    chunk = patch // clips
    dma = pltpu.SemaphoreType.DMA
    anywhere = pl.BlockSpec(memory_space=pl.ANY)
    edge = pltpu.VMEM((chans, frames * pixels), F32)
    x, x_own, weights = pl.pallas_call(
        functools.partial(front_kernel, (frames, width, chans, peers, clips)),
        out_shape=(
            jax.ShapeDtypeStruct((2 * peers * tokens, LANES), BF16),
            jax.ShapeDtypeStruct((2 * tokens, LANES), BF16),
            jax.ShapeDtypeStruct((peers, LANES, 3 * part), BF16),
        ),
        in_specs=[pl.BlockSpec(memory_space=pltpu.SMEM), VMEM] + [anywhere] * 9,
        out_specs=(VMEM,) * 3,
        scratch_shapes=[
            pltpu.VMEM(weight.shape, BF16), pltpu.VMEM((patch, share), BF16), pltpu.VMEM((1, share), F32),
            pltpu.VMEM((TFEAT, share), BF16), pltpu.VMEM(features.shape, BF16), pltpu.VMEM(enc.shape, BF16),
            pltpu.VMEM(time_weight.shape, BF16), pltpu.VMEM(noise.shape, F32), pltpu.VMEM(embed_weight.shape, BF16),
            dma((9,)), pltpu.VMEM((8, TFEAT), F32),
            pltpu.VMEM((clips, 8, TFEAT), F32), dma((clips - 1,)), dma((clips - 1,)),
            edge, edge, edge, dma((2,)), dma((2,)),
            pltpu.VMEM((clips, chunk, 3 * part), BF16), pltpu.VMEM((clips - 1, chunk, 3 * part), BF16),
            pltpu.VMEM((clips, 2, 3 * part), F32), pltpu.VMEM((clips - 1, 2, 3 * part), F32),
            dma((clips - 1,)), dma((clips - 1,)), dma((clips - 1,)), dma((clips - 1,)),
            pltpu.VMEM((peers, 2, tokens, LANES), BF16), dma((peers - 1,)), dma((peers - 1,)),
            pltpu.VMEM((clips, peers, chunk, 3 * part), BF16), pltpu.VMEM((peers, 2, 3 * part), F32),
            dma((peers - 1,)), dma((peers - 1,)), dma((peers - 1,)), dma((peers - 1,)),
            dma((clips // 2,)), dma((clips // 2,)), dma((clips // 2,)), dma((clips // 2,)),
        ],
        compiler_params=pltpu.CompilerParams(collective_id=0, has_side_effects=True),
        name="front",
    )(flow_times, source, weight, embed_cut, gain, time_cut, features, enc, time_weight, noise, embed_weight)
    output, output_t = attend(x, x_own, weights, peers * part)
    return output[None], output_t[None]


def solution(mesh):
    placed = (
        P("clip", None, "seq", None, None),
        P(),
        P("clip", None, "seq", None, None),
        P("clip", None),
        P(),
        P(),
        P(),
        P("clip", None, "seq"),
    )
    return jax.shard_map(
        local,
        mesh=mesh,
        in_specs=placed,
        out_specs=(P("clip", "seq", None), P("clip", "seq", None)),
        check_vma=False,
    )
```
